256 devices in a mesh: seq: 64 (over z, y_hi, x), tp: 4 (over y_lo, core).
Axes of the slice: x: 4, y: 4 (y_hi: 2, y_lo: 2; y = y_hi * 2 + y_lo), z: 8, core: 2. Of those that a mesh axis runs over, the one named last changes fastest.
Arguments:
- queries: bfloat16 [16384, 8192], P('seq', 'tp'), may hold values from -150 to 150
- new_key_value: bfloat16 [2, 16384, 1024], P(None, 'seq', 'tp'), may hold values from -6 to 6
- page_slot: int32 [2048], P('seq'), may hold values from 0 to 2047, as said below
Outputs:
- attended: bfloat16 [16384, 8192], P('seq', 'tp')
- kv_pool: bfloat16 [2, 2048, 8, 1024], P(None, 'seq', None, 'tp')
The draws below stay inside these ranges and needn't reach their ends.
Inputs may be any that keep to these rules, and one draw needn't show every extreme that they name: `page_slot`: each of the 2048 pool slots is named by exactly one page; slots k * 32 to (k + 1) * 32 - 1 are held by index k of seq. The 32 pages of one sequence block go to 32 different owners, one page to each; for each position j of a page within its block, the j-th pages of all blocks go to different owners.
All inputs are finite; a program needn't handle non-finite values.
Results may differ from the reference program's by a relative error of at most 0.0055.
Values may be sent and summed in bfloat16 or wider, within the bound.
A program may use at most 64 MiB of HBM per device.

```python
import math
import jax
import jax.numpy as jnp
from jax import lax

QUERY_HEADS = 64
KEY_VALUE_HEADS = 8
HEAD_SIZE = 128
PAGE_TOKENS = 8
STEPS = 7
BLOCK_TOKENS = 256
SEQUENCE_TOKENS = 16384
PAGES_DEV = 32
PAGE_COUNT = 2048
N_SEQ = 64


def attention_draw(key):
    query_group = QUERY_HEADS // KEY_VALUE_HEADS
    key_rows = jnp.clip(jax.random.normal(jax.random.fold_in(key, 11), (SEQUENCE_TOKENS, KEY_VALUE_HEADS, HEAD_SIZE), jnp.float32), -6.0, 6.0)
    value_rows = jnp.clip(jax.random.normal(jax.random.fold_in(key, 12), (SEQUENCE_TOKENS, KEY_VALUE_HEADS, HEAD_SIZE), jnp.float32), -6.0, 6.0)
    queries = jnp.clip(jax.random.normal(jax.random.fold_in(key, 13), (SEQUENCE_TOKENS, KEY_VALUE_HEADS, query_group, HEAD_SIZE), jnp.float32), -6.0, 6.0)
    return (queries.reshape(SEQUENCE_TOKENS, QUERY_HEADS * HEAD_SIZE), jnp.stack([key_rows, value_rows]).reshape(2, SEQUENCE_TOKENS, KEY_VALUE_HEADS * HEAD_SIZE))


def draw_queries(key, part):
    return attention_draw(key)[0].astype(jnp.bfloat16)


def draw_new_key_value(key, part):
    return attention_draw(key)[1].astype(jnp.bfloat16)


def draw_page_slot(key, part):
    owners = PAGE_COUNT // PAGES_DEV
    per_owner = (PAGES_DEV + owners - 1) // owners
    named = PAGES_DEV // per_owner
    order = jax.random.permutation(jax.random.fold_in(key, 21), owners)
    offset = jax.random.permutation(jax.random.fold_in(key, 22), owners)[:named]
    source = jnp.arange(owners)[:, None]
    column = jnp.broadcast_to(jnp.arange(PAGES_DEV)[None, :], (owners, PAGES_DEV))
    owner = order[(source + offset[column // per_owner]) % owners]
    slot_keys = jax.random.split(jax.random.fold_in(key, 23), owners)
    arrangement = jax.vmap(lambda single: jax.random.permutation(single, PAGES_DEV))(slot_keys)
    within = arrangement[owner, column]
    return (owner * PAGES_DEV + within).reshape(-1).astype(jnp.int32)


def setup_inputs(seed: int = 0) -> dict:
    splits = jax.random.split(jax.random.key(seed), 4)
    return {
        "queries": draw_queries(jax.random.fold_in(splits[3], 71), 0),
        "new_key_value": draw_new_key_value(jax.random.fold_in(splits[3], 71), 0),
        "page_slot": draw_page_slot(jax.random.fold_in(splits[3], 71), 0),
    }


masked_score = -1e+30

def attend_all(queries, new_key_value):
    query_group = QUERY_HEADS // KEY_VALUE_HEADS
    query_block_rows = queries.reshape(N_SEQ, BLOCK_TOKENS, KEY_VALUE_HEADS, query_group, HEAD_SIZE)
    key_rows = new_key_value[0].reshape(SEQUENCE_TOKENS, KEY_VALUE_HEADS, HEAD_SIZE)
    value_rows = new_key_value[1].reshape(SEQUENCE_TOKENS, KEY_VALUE_HEADS, HEAD_SIZE)
    window_margin = (STEPS - 1) * BLOCK_TOKENS
    key_rows = jnp.concatenate([jnp.zeros((window_margin, KEY_VALUE_HEADS, HEAD_SIZE), key_rows.dtype), key_rows], 0)
    value_rows = jnp.concatenate([jnp.zeros((window_margin, KEY_VALUE_HEADS, HEAD_SIZE), value_rows.dtype), value_rows], 0)
    scale = 1.0 / math.sqrt(HEAD_SIZE)

    def one_block(index):
        query_part = lax.dynamic_index_in_dim(query_block_rows, index, 0, keepdims=False).astype(jnp.float32)
        start = (index * BLOCK_TOKENS).astype(jnp.int32)
        key_part = lax.dynamic_slice_in_dim(key_rows, start, STEPS * BLOCK_TOKENS, 0).astype(jnp.float32)
        value_part = lax.dynamic_slice_in_dim(value_rows, start, STEPS * BLOCK_TOKENS, 0).astype(jnp.float32)
        score = jnp.einsum('ikgd,jkd->kgij', query_part, key_part) * scale
        query_pos = index * BLOCK_TOKENS + jnp.arange(BLOCK_TOKENS, dtype=jnp.int32)
        key_pos = (index - STEPS + 1) * BLOCK_TOKENS + jnp.arange(STEPS * BLOCK_TOKENS, dtype=jnp.int32)
        valid = (key_pos[None, :] >= 0) & (key_pos[None, :] <= query_pos[:, None])
        score = jnp.where(valid, score, masked_score)
        top = lax.optimization_barrier(jnp.max(score, -1, keepdims=True))
        weight = jnp.where(valid, jnp.exp(score - top), 0.0)
        total = lax.optimization_barrier(jnp.sum(weight, -1))
        rounded = lax.optimization_barrier(weight.astype(jnp.bfloat16)).astype(jnp.float32)
        mixed = jnp.einsum('kgij,jkd->ikgd', rounded, value_part)
        result = mixed / jnp.transpose(total, (2, 0, 1))[..., None]
        return result.astype(jnp.bfloat16).reshape(BLOCK_TOKENS, QUERY_HEADS * HEAD_SIZE)
    blocks = lax.map(one_block, jnp.arange(N_SEQ, dtype=jnp.int32))
    return blocks.reshape(SEQUENCE_TOKENS, QUERY_HEADS * HEAD_SIZE)

def reference(queries, new_key_value, page_slot):
    attended = attend_all(queries, new_key_value)
    page_table = new_key_value.reshape(2, PAGE_COUNT, PAGE_TOKENS, KEY_VALUE_HEADS * HEAD_SIZE)
    kv_pool = jnp.zeros_like(page_table).at[:, page_slot].set(page_table)
    return (attended, kv_pool)
```

```python
import functools
import math

import jax
import jax.numpy as jnp
from jax import lax
from jax.experimental import pallas as pl
from jax.experimental.pallas import tpu as pltpu
from jax.sharding import PartitionSpec as P

MESH = pl.DeviceIdType.MESH
HEAD = 128
GROUP = 8
NX, NH, NZ = 4, 2, 8
NP = NX * NH
PAGES = 32
PAGE = 8
F32 = jnp.float32
BF16 = jnp.bfloat16
LOW = -1e30

A, B, C, D, E, F, G, O3, O2 = range(9)


def kernel(
    slot_ref, q_hbm, kv_hbm, o_ref, pool_ref,
    q_buf, own, kvb, acc, top, pick, sbuf, zbuf, pbuf, row, tab1, tab2, place,
    q_sem, own_sem, loc_sem, kv_recv, kv_send,
    z_recv, z_send, zt_recv, zt_send, p_recv, p_send, pt_recv, pt_send,
):
    s = lax.axis_index("seq")
    tp = lax.axis_index("tp")
    z, p = s // NP, s % NP
    h, x = p // NX, p % NX
    n_seq = NP * NZ
    right = s - x + lax.rem(x + 1, NX)
    left = s - x + lax.rem(x + NX - 1, NX)
    row_up = lax.rem(s + NX, n_seq)
    z_up = lax.rem(s + NP, n_seq)

    own_copy = pltpu.make_async_copy(kv_hbm, own, own_sem)
    own_copy.start()
    heads = q_buf.shape[0]
    q_copies = [
        pltpu.make_async_copy(q_hbm.at[:, pl.ds(i * HEAD, HEAD)], q_buf.at[i], q_sem.at[i])
        for i in range(heads)
    ]
    for copy in q_copies:
        copy.start()

    barrier = pltpu.get_barrier_semaphore()

    def greet(device):
        pl.semaphore_signal(barrier, inc=1, device_id=(device, tp), device_id_type=MESH)

    z_peers = [lax.rem(z + k, NZ) for k in range(1, NZ)]
    p_peers = [lax.rem(p + k, NP) for k in range(1, NP)]
    for peer in z_peers:
        greet(peer * NP + p)
    for peer in p_peers:
        greet(z * NP + peer)
    greet(lax.rem(jnp.where(h == 0, s - NX, s + NX) + n_seq, n_seq))

    lane = lax.broadcasted_iota(jnp.int32, (PAGE, n_seq * PAGE), 1)
    sub = lax.broadcasted_iota(jnp.int32, (PAGE, n_seq * PAGE), 0)
    same_token = (lane % PAGE) == sub
    lane_owner = lane // PAGE
    narrow = lax.broadcasted_iota(jnp.int32, (1, 128), 1)
    slots = jnp.full((1, 128), -1, jnp.int32)
    for j in range(PAGES):
        slot = slot_ref[j]
        pick[j * PAGE : (j + 1) * PAGE, :] = jnp.where(
            jnp.logical_and(same_token, lane_owner == slot // PAGES), 1.0, 0.0
        ).astype(BF16)
        slots = jnp.where(narrow == j, slot, slots)
    row[...] = slots
    own_copy.wait()
    for c in range(2):
        outgoing = lax.dot_general(
            pick[...], own[c], (((0,), (0,)), ((), ())), preferred_element_type=F32
        )
        sbuf[:, :, c * PAGE : (c + 1) * PAGE, :] = outgoing.astype(BF16).reshape(NZ, NP, PAGE, -1)

    pl.semaphore_wait(barrier, NZ - 1 + NP - 1 + 1)

    def hop(src, slot, c, device, number):
        return pltpu.make_async_remote_copy(
            src_ref=src.at[c], dst_ref=kvb.at[slot, c],
            send_sem=kv_send.at[number, c], recv_sem=kv_recv.at[slot, c],
            device_id=(device, tp), device_id_type=MESH,
        )

    def arrived(slot, c):
        hop(kvb.at[slot], slot, c, right, 0).wait_recv()

    last = x == NX - 1
    first = x == 0
    rows_up = [hop(own, C, c, row_up, 0) for c in range(2)]
    old3 = [hop(own, O3, c, z_up, 1) for c in range(2)]
    step1 = [hop(own, A, c, right, 2) for c in range(2)]
    step1_old = [hop(kvb.at[O3], A, c, right, 2) for c in range(2)]
    extra = [hop(own, G, c, left, 3) for c in range(2)]
    old2 = [hop(kvb.at[A], O2, c, z_up, 4) for c in range(2)]
    step2 = [hop(kvb.at[A], B, c, right, 5) for c in range(2)]
    step2_old = [hop(kvb.at[O2], B, c, right, 5) for c in range(2)]
    to_right = [hop(kvb.at[C], D, c, right, 6) for c in range(2)]
    to_left = [hop(kvb.at[C], E, c, left, 7) for c in range(2)]
    to_left2 = [hop(kvb.at[E], F, c, left, 8) for c in range(2)]

    for c in range(2):
        rows_up[c].start()
        pl.when(last)(old3[c].start)
        pl.when(jnp.logical_not(last))(step1[c].start)
        pl.when(first)(extra[c].start)

    stage1 = []
    for k, peer in enumerate(z_peers):
        device = (peer * NP + p, tp)
        stage1.append(pltpu.make_async_remote_copy(
            src_ref=sbuf.at[peer], dst_ref=zbuf.at[:, z], send_sem=z_send.at[k], recv_sem=z_recv.at[z],
            device_id=device, device_id_type=MESH))
        stage1.append(pltpu.make_async_remote_copy(
            src_ref=row, dst_ref=tab1.at[z], send_sem=zt_send.at[k], recv_sem=zt_recv.at[z],
            device_id=device, device_id_type=MESH))
    for copy in stage1:
        copy.start()
    loc1 = pltpu.make_async_copy(sbuf.at[z], zbuf.at[:, z], loc_sem.at[0])
    loc2 = pltpu.make_async_copy(row, tab1.at[z], loc_sem.at[1])
    loc1.start()
    loc2.start()
    for copy in q_copies:
        copy.wait()

    to_exp2 = math.log2(math.e) / math.sqrt(HEAD)
    ones = jnp.ones((own.shape[1], HEAD), BF16)
    tokens = own.shape[1]
    heads_kv = heads // GROUP

    def absorb(block, initial):
        for g in range(heads_kv):
            keys = block[0, :, g * HEAD : (g + 1) * HEAD]
            values = jnp.concatenate([block[1, :, g * HEAD : (g + 1) * HEAD], ones], axis=1)

            def one(i, _):
                head = g * GROUP + i
                score = lax.dot_general(
                    q_buf[head], keys, (((1,), (1,)), ((), ())), preferred_element_type=F32
                ) * to_exp2
                if initial:
                    causal = lax.broadcasted_iota(jnp.int32, (tokens, tokens), 1) <= lax.broadcasted_iota(
                        jnp.int32, (tokens, tokens), 0)
                    score = jnp.where(causal, score, LOW)
                    new_top = jnp.max(score, axis=1, keepdims=True)
                else:
                    new_top = jnp.maximum(top[head][:, :1], jnp.max(score, axis=1, keepdims=True))
                weight = jnp.exp2(score - new_top).astype(BF16)
                mixed = jnp.dot(weight, values, preferred_element_type=F32)
                if initial:
                    acc[head] = mixed
                else:
                    acc[head] = acc[head] * jnp.exp2(top[head][:, :1] - new_top) + mixed
                top[head] = jnp.broadcast_to(new_top, (tokens, HEAD))
                return 0

            lax.fori_loop(0, GROUP, one, 0)

    def absorb_slot(slot, distance):
        pl.when(s >= distance)(lambda: absorb(kvb.at[slot], False))

    absorb(own, True)

    @pl.when(last)
    def _():
        for c in range(2):
            arrived(O3, c)
            step1_old[c].start()

    @pl.when(jnp.logical_not(first))
    def _():
        for c in range(2):
            arrived(A, c)
            pl.when(last)(old2[c].start)
            pl.when(jnp.logical_not(last))(step2[c].start)

    for c in range(2):
        arrived(C, c)
        to_left[c].start()
        to_right[c].start()

    absorb_slot(C, 4)

    @pl.when(first)
    def _():
        for c in range(2):
            arrived(A, c)
            step2[c].start()

    @pl.when(last)
    def _():
        for c in range(2):
            arrived(O2, c)
            step2_old[c].start()

    for c in range(2):
        arrived(E, c)
        to_left2[c].start()

    absorb_slot(A, jnp.where(first, 5, 1))

    for k, peer in enumerate(z_peers):
        pltpu.make_async_remote_copy(
            src_ref=sbuf.at[peer], dst_ref=zbuf.at[:, peer], send_sem=z_send.at[k], recv_sem=z_recv.at[peer],
            device_id=(right, tp), device_id_type=MESH).wait_recv()
        pltpu.make_async_remote_copy(
            src_ref=row, dst_ref=tab1.at[peer], send_sem=zt_send.at[k], recv_sem=zt_recv.at[peer],
            device_id=(right, tp), device_id_type=MESH).wait_recv()
    loc1.wait()
    loc2.wait()
    stage2 = []
    for k, peer in enumerate(p_peers):
        device = (z * NP + peer, tp)
        stage2.append(pltpu.make_async_remote_copy(
            src_ref=zbuf.at[peer], dst_ref=pbuf.at[p], send_sem=p_send.at[k], recv_sem=p_recv.at[p],
            device_id=device, device_id_type=MESH))
        stage2.append(pltpu.make_async_remote_copy(
            src_ref=tab1, dst_ref=tab2.at[p], send_sem=pt_send.at[k], recv_sem=pt_recv.at[p],
            device_id=device, device_id_type=MESH))
    for copy in stage2:
        copy.start()
    loc3 = pltpu.make_async_copy(zbuf.at[p], pbuf.at[p], loc_sem.at[2])
    loc4 = pltpu.make_async_copy(tab1, tab2.at[p], loc_sem.at[3])
    loc3.start()
    loc4.start()

    @pl.when(last)
    def _():
        for c in range(2):
            arrived(G, c)

    absorb_slot(jnp.where(last, G, E), 3)
    for c in range(2):
        arrived(D, c)
    absorb_slot(D, jnp.where(first, 1, 5))
    for c in range(2):
        arrived(B, c)
    absorb_slot(B, jnp.where(x >= 2, 2, 6))
    for c in range(2):
        arrived(F, c)
    absorb_slot(F, jnp.where(x < 2, 2, 6))

    for k, peer in enumerate(p_peers):
        pltpu.make_async_remote_copy(
            src_ref=zbuf.at[peer], dst_ref=pbuf.at[peer], send_sem=p_send.at[k], recv_sem=p_recv.at[peer],
            device_id=(right, tp), device_id_type=MESH).wait_recv()
        pltpu.make_async_remote_copy(
            src_ref=tab1, dst_ref=tab2.at[peer], send_sem=pt_send.at[k], recv_sem=pt_recv.at[peer],
            device_id=(right, tp), device_id_type=MESH).wait_recv()
    loc3.wait()
    loc4.wait()
    wide = lax.broadcasted_iota(jnp.int32, (PAGE, PAGES * PAGE), 1)
    wide_token = (wide % PAGE) == lax.broadcasted_iota(jnp.int32, (PAGE, PAGES * PAGE), 0)
    wide_slot = wide // PAGE
    for source in range(n_seq):
        named = jnp.broadcast_to(tab2[source // NZ, source % NZ], (PAGE, 128))
        mine = jnp.where(named // PAGES == s, named % PAGES + 1, 0)
        within = jnp.sum(mine, axis=1, keepdims=True) - 1
        place[source * PAGE : (source + 1) * PAGE, :] = jnp.where(
            jnp.logical_and(wide_token, wide_slot == within), 1.0, 0.0
        ).astype(BF16)
    for c in range(2):
        pages = pbuf[:, :, c * PAGE : (c + 1) * PAGE, :].reshape(n_seq * PAGE, -1)
        pool_ref[c] = lax.dot_general(
            place[...], pages, (((0,), (0,)), ((), ())), preferred_element_type=F32
        ).astype(BF16)

    for i in range(heads):
        o_ref[:, i * HEAD : (i + 1) * HEAD] = (acc[i, :, :HEAD] / acc[i, :, HEAD:]).astype(BF16)

    for c in range(2):
        rows_up[c].wait_send()
        step1[c].wait_send()
        step2[c].wait_send()
        to_right[c].wait_send()
        to_left[c].wait_send()
        to_left2[c].wait_send()
        pl.when(last)(old3[c].wait_send)
        pl.when(last)(old2[c].wait_send)
        pl.when(first)(extra[c].wait_send)
    for copy in stage1 + stage2:
        copy.wait_send()


def body(queries, new_key_value, page_slot):
    tokens, features = queries.shape
    width = new_key_value.shape[2]
    heads = features // HEAD
    n_seq = NP * NZ
    kv_block = (2, tokens, width)
    dma = pltpu.SemaphoreType.DMA
    attended, pool = pl.pallas_call(
        kernel,
        name="layer",
        out_shape=(
            jax.ShapeDtypeStruct((tokens, features), BF16),
            jax.ShapeDtypeStruct(kv_block, BF16),
        ),
        in_specs=[
            pl.BlockSpec(memory_space=pltpu.SMEM),
            pl.BlockSpec(memory_space=pl.ANY),
            pl.BlockSpec(memory_space=pl.ANY),
        ],
        out_specs=(
            pl.BlockSpec(memory_space=pltpu.VMEM),
            pl.BlockSpec(memory_space=pltpu.VMEM),
        ),
        scratch_shapes=[
            pltpu.VMEM((heads, tokens, HEAD), BF16),
            pltpu.VMEM(kv_block, BF16),
            pltpu.VMEM((9,) + kv_block, BF16),
            pltpu.VMEM((heads, tokens, 2 * HEAD), F32),
            pltpu.VMEM((heads, tokens, HEAD), F32),
            pltpu.VMEM((PAGES * PAGE, n_seq * PAGE), BF16),
            pltpu.VMEM((NZ, NP, 2 * PAGE, width), BF16),
            pltpu.VMEM((NP, NZ, 2 * PAGE, width), BF16),
            pltpu.VMEM((NP, NZ, 2 * PAGE, width), BF16),
            pltpu.VMEM((1, 128), jnp.int32),
            pltpu.VMEM((NZ, 1, 128), jnp.int32),
            pltpu.VMEM((NP, NZ, 1, 128), jnp.int32),
            pltpu.VMEM((n_seq * PAGE, PAGES * PAGE), BF16),
            dma((heads,)), dma, dma((4,)), dma((9, 2)), dma((9, 2)),
            dma((NZ,)), dma((NZ,)), dma((NZ,)), dma((NZ,)),
            dma((NP,)), dma((NP,)), dma((NP,)), dma((NP,)),
        ],
        compiler_params=pltpu.CompilerParams(
            collective_id=0, has_side_effects=True, vmem_limit_bytes=48 << 20
        ),
    )(page_slot, queries, new_key_value)
    return attended, pool.reshape(2, PAGES, PAGE, width)


def solution(mesh):
    return jax.shard_map(
        body,
        mesh=mesh,
        in_specs=(P("seq", "tp"), P(None, "seq", "tp"), P("seq")),
        out_specs=(P("seq", "tp"), P(None, "seq", None, "tp")),
        check_vma=False,
    )
```

```python
import functools
import math

import jax
import jax.numpy as jnp
from jax import lax
from jax.experimental import pallas as pl
from jax.experimental.pallas import tpu as pltpu
from jax.sharding import PartitionSpec as P

MESH = pl.DeviceIdType.MESH
HEAD = 128
GROUP = 8
NX, NH, NZ = 4, 2, 8
NP = NX * NH
PAGES = 32
PAGE = 8
F32 = jnp.float32
BF16 = jnp.bfloat16
LOW = -1e30

A, B, C, D, E, F, G, O, O2 = range(9)


def kernel(
    slot_ref, q_hbm, kv_hbm, o_ref, pool_ref,
    q_buf, own, kvb, acc, top, mix, pick, send_k, send_v, mid_k, mid_v, got_k, got_v, row, tab1, tab2, place,
    q_sem, own_sem, loc_sem, kv_recv, kv_send,
    k1_recv, k1_send, v1_recv, v1_send, k2_recv, k2_send, v2_recv, v2_send,
    t1_recv, t1_send, t2_recv, t2_send,
):
    s = lax.axis_index("seq")
    tp = lax.axis_index("tp")
    z, p = s // NP, s % NP
    h, x = p // NX, p % NX
    n_seq = NP * NZ
    right = s - x + lax.rem(x + 1, NX)
    left = s - x + lax.rem(x + NX - 1, NX)
    row_up = lax.rem(s + NX, n_seq)
    z_up = lax.rem(s + NP, n_seq)

    own_copy = pltpu.make_async_copy(kv_hbm, own, own_sem)
    own_copy.start()
    heads = q_buf.shape[0]
    q_copies = [
        pltpu.make_async_copy(q_hbm.at[:, pl.ds(i * HEAD, HEAD)], q_buf.at[i], q_sem.at[i])
        for i in range(heads)
    ]
    for copy in q_copies:
        copy.start()

    barrier = pltpu.get_barrier_semaphore()

    def greet(device):
        pl.semaphore_signal(barrier, inc=1, device_id=(device, tp), device_id_type=MESH)

    z_peers = [lax.rem(z + k, NZ) for k in range(1, NZ)]
    p_peers = [lax.rem(p + k, NP) for k in range(1, NP)]
    for peer in z_peers:
        greet(peer * NP + p)
    for peer in p_peers:
        greet(z * NP + peer)
    greet(lax.rem(jnp.where(h == 0, s - NX, s + NX) + n_seq, n_seq))

    def remote(src, dst, send_sem, recv_sem, device):
        return pltpu.make_async_remote_copy(
            src_ref=src, dst_ref=dst, send_sem=send_sem, recv_sem=recv_sem,
            device_id=(device, tp), device_id_type=MESH,
        )

    half = own.shape[1] // 2
    parts = [(c, pl.ds(i * half, half)) for c in range(2) for i in range(2)]

    def hop(src, slot, device, number):
        return [
            remote(src.at[part], kvb.at[(slot,) + part], kv_send.at[number, k], kv_recv.at[slot, k], device)
            for k, part in enumerate(parts)
        ]

    def arrived(slot, k):
        hop(kvb.at[slot], slot, right, 0)[k].wait_recv()

    first = x == 0
    last = x == NX - 1
    upper = x >= NX // 2
    rows_up = hop(own, C, row_up, 0)
    to_z = hop(kvb.at[O], A, z_up, 1)
    step1 = hop(own, A, right, 2)
    step1_last = hop(own, O, right, 2)
    extra = hop(own, G, left, 3)
    step2 = hop(kvb.at[A], B, right, 4)
    to_z2 = hop(kvb.at[A], O2, z_up, 8)
    step2_old = hop(kvb.at[O2], B, right, 4)
    to_right = hop(kvb.at[C], D, right, 5)
    to_left = hop(kvb.at[C], E, left, 6)
    to_left2 = hop(kvb.at[E], F, left, 7)

    own_copy.wait()
    pl.semaphore_wait(barrier, NZ - 1 + NP - 1 + 1)
    for k in range(4):
        rows_up[k].start()
        pl.when(last)(step1_last[k].start)
        pl.when(jnp.logical_not(last))(step1[k].start)
        pl.when(first)(extra[k].start)

    lane = lax.broadcasted_iota(jnp.int32, (PAGE, n_seq * PAGE), 1)
    sub = lax.broadcasted_iota(jnp.int32, (PAGE, n_seq * PAGE), 0)
    same_token = (lane % PAGE) == sub
    lane_owner = lane // PAGE
    narrow = lax.broadcasted_iota(jnp.int32, (1, 128), 1)
    slots = jnp.full((1, 128), -1, jnp.int32)
    for j in range(PAGES):
        slot = slot_ref[j]
        pick[j * PAGE : (j + 1) * PAGE, :] = jnp.where(
            jnp.logical_and(same_token, lane_owner == slot // PAGES), 1.0, 0.0
        ).astype(BF16)
        slots = jnp.where(narrow == j, slot, slots)
    row[...] = slots
    for c, outgoing in ((0, send_k), (1, send_v)):
        outgoing[...] = lax.dot_general(
            pick[...], own[c], (((0,), (0,)), ((), ())), preferred_element_type=F32
        ).astype(BF16).reshape(NZ, NP, PAGE, -1)

    stage2 = []

    def start_values():
        for copy in stage1_v:
            copy.start()

    def pass_values():
        for k, peer in enumerate(p_peers):
            remote(send_v.at[:, peer], mid_v.at[:, peer], v1_send.at[k], v1_recv.at[peer], right).wait_recv()
        local1[2].wait()
        local2[0].start()
        for k, peer in enumerate(z_peers):
            stage2.append(remote(mid_v.at[peer], got_v.at[:, z], v2_send.at[k], v2_recv.at[z], peer * NP + p))
            stage2[-1].start()

    def pass_keys():
        for k, peer in enumerate(z_peers):
            remote(send_k.at[peer], mid_k.at[:, peer], k1_send.at[k], k1_recv.at[peer], right).wait_recv()
            remote(row, tab1.at[peer], t1_send.at[k], t1_recv.at[peer], right).wait_recv()
        local1[0].wait()
        local1[1].wait()
        local2[1].start()
        local2[2].start()
        for k, peer in enumerate(p_peers):
            stage2.append(remote(mid_k.at[peer], got_k.at[p], k2_send.at[k], k2_recv.at[p], z * NP + peer))
            stage2[-1].start()
            stage2.append(remote(tab1, tab2.at[p], t2_send.at[k], t2_recv.at[p], z * NP + peer))
            stage2[-1].start()

    local2 = [
        pltpu.make_async_copy(mid_v.at[z], got_v.at[:, z], loc_sem.at[3]),
        pltpu.make_async_copy(mid_k.at[p], got_k.at[p], loc_sem.at[4]),
        pltpu.make_async_copy(tab1, tab2.at[p], loc_sem.at[5]),
    ]
    stage1 = []
    for k, peer in enumerate(z_peers):
        stage1.append(remote(send_k.at[peer], mid_k.at[:, z], k1_send.at[k], k1_recv.at[z], peer * NP + p))
        stage1.append(remote(row, tab1.at[z], t1_send.at[k], t1_recv.at[z], peer * NP + p))
    stage1_v = [
        remote(send_v.at[:, peer], mid_v.at[:, p], v1_send.at[k], v1_recv.at[p], z * NP + peer)
        for k, peer in enumerate(p_peers)
    ]
    local1 = [
        pltpu.make_async_copy(send_k.at[z], mid_k.at[:, z], loc_sem.at[0]),
        pltpu.make_async_copy(row, tab1.at[z], loc_sem.at[1]),
        pltpu.make_async_copy(send_v.at[:, p], mid_v.at[:, p], loc_sem.at[2]),
    ]
    for copy in stage1 + local1:
        copy.start()
    start_values()
    for copy in q_copies:
        copy.wait()

    to_exp2 = math.log2(math.e) / math.sqrt(HEAD)
    tokens = own.shape[1]
    heads_kv = heads // GROUP

    def absorb(block, initial):
        for g in range(heads_kv):
            mix[g, :, :HEAD] = block[1, :, g * HEAD : (g + 1) * HEAD]

            def one(i, _):
                head = g * GROUP + i
                score = lax.dot_general(
                    q_buf[head], block[0, :, g * HEAD : (g + 1) * HEAD],
                    (((1,), (1,)), ((), ())), preferred_element_type=F32,
                ) * to_exp2
                if initial:
                    causal = lax.broadcasted_iota(jnp.int32, (tokens, tokens), 1) <= lax.broadcasted_iota(
                        jnp.int32, (tokens, tokens), 0)
                    score = jnp.where(causal, score, LOW)
                    new_top = jnp.broadcast_to(jnp.max(score, axis=1, keepdims=True), (tokens, HEAD))
                else:
                    old_top = top[head]
                    new_top = jnp.maximum(old_top, jnp.max(score, axis=1, keepdims=True))
                weight = jnp.exp2(score - jnp.concatenate([new_top, new_top], axis=1)).astype(BF16)
                mixed = jnp.dot(weight, mix[g], preferred_element_type=F32)
                top[head] = new_top
                if initial:
                    acc[head] = mixed
                else:
                    fade = jnp.exp2(old_top - new_top)
                    acc[head] = acc[head] * jnp.concatenate([fade, fade], axis=1) + mixed
                return 0

            lax.fori_loop(0, GROUP, one, 0, unroll=True)

    def absorb_slot(slot, distance):
        pl.when(s >= distance)(lambda: absorb(kvb.at[slot], False))

    mix[:, :, HEAD:] = jnp.ones((heads_kv, tokens, HEAD), BF16)
    absorb(own, True)

    def from_row(k):
        arrived(C, k)
        to_left[k].start()
        to_right[k].start()

    for k in range(4):
        @pl.when(first)
        def _():
            arrived(O, k)
            to_z[k].start()

        @pl.when(jnp.logical_not(first))
        def _():
            arrived(A, k)
            pl.when(last)(to_z2[k].start)
            pl.when(jnp.logical_not(last))(step2[k].start)

        if k >= 1:
            from_row(k - 1)
    from_row(3)

    pass_values()
    pass_keys()
    absorb_slot(C, 4)

    for k in range(4):
        @pl.when(first)
        def _():
            arrived(A, k)
            step2[k].start()

        @pl.when(last)
        def _():
            arrived(O2, k)
            step2_old[k].start()

        arrived(E, k)
        to_left2[k].start()

    absorb_slot(A, jnp.where(first, 5, 1))

    @pl.when(last)
    def _():
        for k in range(4):
            arrived(G, k)

    absorb_slot(jnp.where(last, G, E), 3)
    for slot, distance in (
        (B, jnp.where(upper, 2, 6)),
        (D, jnp.where(first, 1, 5)),
        (F, jnp.where(upper, 6, 2)),
    ):
        for k in range(4):
            arrived(slot, k)
        absorb_slot(slot, distance)

    for i in range(heads):
        o_ref[:, i * HEAD : (i + 1) * HEAD] = (acc[i, :, :HEAD] / acc[i, :, HEAD:]).astype(BF16)

    for k, peer in enumerate(z_peers):
        remote(mid_v.at[peer], got_v.at[:, peer], v2_send.at[k], v2_recv.at[peer], right).wait_recv()
    for k, peer in enumerate(p_peers):
        remote(mid_k.at[peer], got_k.at[peer], k2_send.at[k], k2_recv.at[peer], right).wait_recv()
        remote(tab1, tab2.at[peer], t2_send.at[k], t2_recv.at[peer], right).wait_recv()
    for copy in local2:
        copy.wait()
    wide = lax.broadcasted_iota(jnp.int32, (PAGE, PAGES * PAGE), 1)
    wide_token = (wide % PAGE) == lax.broadcasted_iota(jnp.int32, (PAGE, PAGES * PAGE), 0)
    wide_slot = wide // PAGE
    for source in range(n_seq):
        named = jnp.broadcast_to(tab2[source // NZ, source % NZ], (PAGE, 128))
        mine = jnp.where(named // PAGES == s, named % PAGES + 1, 0)
        within = jnp.sum(mine, axis=1, keepdims=True) - 1
        place[source * PAGE : (source + 1) * PAGE, :] = jnp.where(
            jnp.logical_and(wide_token, wide_slot == within), 1.0, 0.0
        ).astype(BF16)
    for c, pages in ((0, got_k), (1, got_v)):
        pool_ref[c] = lax.dot_general(
            place[...], pages[...].reshape(n_seq * PAGE, -1), (((0,), (0,)), ((), ())), preferred_element_type=F32
        ).astype(BF16)

    for k in range(4):
        rows_up[k].wait_send()
        pl.when(first)(to_z[k].wait_send)
        pl.when(last)(to_z2[k].wait_send)
        step1[k].wait_send()
        pl.when(first)(extra[k].wait_send)
        step2[k].wait_send()
        to_right[k].wait_send()
        to_left[k].wait_send()
        to_left2[k].wait_send()
    for copy in stage1 + stage1_v + stage2:
        copy.wait_send()


def body(queries, new_key_value, page_slot):
    tokens, features = queries.shape
    width = new_key_value.shape[2]
    heads = features // HEAD
    n_seq = NP * NZ
    kv_block = (2, tokens, width)
    dma = pltpu.SemaphoreType.DMA
    attended, pool = pl.pallas_call(
        kernel,
        name="layer",
        out_shape=(
            jax.ShapeDtypeStruct((tokens, features), BF16),
            jax.ShapeDtypeStruct(kv_block, BF16),
        ),
        in_specs=[
            pl.BlockSpec(memory_space=pltpu.SMEM),
            pl.BlockSpec(memory_space=pl.ANY),
            pl.BlockSpec(memory_space=pl.ANY),
        ],
        out_specs=(
            pl.BlockSpec(memory_space=pltpu.VMEM),
            pl.BlockSpec(memory_space=pltpu.VMEM),
        ),
        scratch_shapes=[
            pltpu.VMEM((heads, tokens, HEAD), BF16),
            pltpu.VMEM(kv_block, BF16),
            pltpu.VMEM((9,) + kv_block, BF16),
            pltpu.VMEM((heads, tokens, 2 * HEAD), F32),
            pltpu.VMEM((heads, tokens, HEAD), F32),
            pltpu.VMEM((width // HEAD, tokens, 2 * HEAD), BF16),
            pltpu.VMEM((PAGES * PAGE, n_seq * PAGE), BF16),
            *[pltpu.VMEM((NP, NP, PAGE, width), BF16)] * 6,
            pltpu.VMEM((1, 128), jnp.int32),
            pltpu.VMEM((NZ, 1, 128), jnp.int32),
            pltpu.VMEM((NP, NZ, 1, 128), jnp.int32),
            pltpu.VMEM((n_seq * PAGE, PAGES * PAGE), BF16),
            dma((heads,)), dma, dma((6,)), dma((9, 4)), dma((9, 4)),
            *[dma((NP,))] * 12,
        ],
        compiler_params=pltpu.CompilerParams(
            collective_id=0, has_side_effects=True, vmem_limit_bytes=60 * 1024 * 1024
        ),
    )(page_slot, queries, new_key_value)
    return attended, pool.reshape(2, PAGES, PAGE, width)


def solution(mesh):
    return jax.shard_map(
        body,
        mesh=mesh,
        in_specs=(P("seq", "tp"), P(None, "seq", "tp"), P("seq")),
        out_specs=(P("seq", "tp"), P(None, "seq", None, "tp")),
        check_vma=False,
    )
```

```python
import functools
import math

import jax
import jax.numpy as jnp
from jax import lax
from jax.experimental import pallas as pl
from jax.experimental.pallas import tpu as pltpu
from jax.sharding import PartitionSpec as P

MESH = pl.DeviceIdType.MESH
HEAD = 128
GROUP = 8
NX, NH, NZ = 4, 2, 8
NP = NX * NH
PAGES = 32
PAGE = 8
F32 = jnp.float32
BF16 = jnp.bfloat16
LOW = -1e30

A, B, C, D, E, F, G, O, O2 = range(9)


def kernel(
    slot_ref, q_hbm, kv_hbm, o_ref, pool_ref,
    q_buf, own, kvb, acc, top, mix, pick, send_k, send_v, mid_k, mid_v, got_k, got_v, row, tab1, tab2, place,
    q_sem, own_sem, loc_sem, kv_recv, kv_send,
    k1_recv, k1_send, v1_recv, v1_send, k2_recv, k2_send, v2_recv, v2_send,
    t1_recv, t1_send, t2_recv, t2_send,
):
    s = lax.axis_index("seq")
    tp = lax.axis_index("tp")
    z, p = s // NP, s % NP
    h, x = p // NX, p % NX
    n_seq = NP * NZ
    right = s - x + lax.rem(x + 1, NX)
    left = s - x + lax.rem(x + NX - 1, NX)
    row_up = lax.rem(s + NX, n_seq)
    z_up = lax.rem(s + NP, n_seq)

    own_copy = pltpu.make_async_copy(kv_hbm, own, own_sem)
    own_copy.start()
    heads = q_buf.shape[0]
    q_copies = [
        pltpu.make_async_copy(q_hbm.at[:, pl.ds(i * HEAD, HEAD)], q_buf.at[i], q_sem.at[i])
        for i in range(heads)
    ]
    for copy in q_copies:
        copy.start()

    barrier = pltpu.get_barrier_semaphore()

    def greet(device):
        pl.semaphore_signal(barrier, inc=1, device_id=(device, tp), device_id_type=MESH)

    z_peers = [lax.rem(z + k, NZ) for k in range(1, NZ)]
    p_peers = [lax.rem(p + k, NP) for k in range(1, NP)]
    for peer in z_peers:
        greet(peer * NP + p)
    for peer in p_peers:
        greet(z * NP + peer)
    greet(lax.rem(jnp.where(h == 0, s - NX, s + NX) + n_seq, n_seq))

    def remote(src, dst, send_sem, recv_sem, device):
        return pltpu.make_async_remote_copy(
            src_ref=src, dst_ref=dst, send_sem=send_sem, recv_sem=recv_sem,
            device_id=(device, tp), device_id_type=MESH,
        )

    half = own.shape[1] // 2
    parts = [(c, pl.ds(i * half, half)) for c in range(2) for i in range(2)]

    def hop(src, slot, device, number):
        return [
            remote(src.at[part], kvb.at[(slot,) + part], kv_send.at[number, k], kv_recv.at[slot, k], device)
            for k, part in enumerate(parts)
        ]

    def arrived(slot, k):
        hop(kvb.at[slot], slot, right, 0)[k].wait_recv()

    first = x == 0
    last = x == NX - 1
    upper = x >= NX // 2
    rows_up = hop(own, C, row_up, 0)
    to_z = hop(kvb.at[O], A, z_up, 1)
    step1 = hop(own, A, right, 2)
    step1_last = hop(own, O, right, 2)
    extra = hop(own, G, left, 3)
    step2 = hop(kvb.at[A], B, right, 4)
    to_z2 = hop(kvb.at[A], O2, z_up, 8)
    step2_old = hop(kvb.at[O2], B, right, 4)
    to_right = hop(kvb.at[C], D, right, 5)
    to_left = hop(kvb.at[C], E, left, 6)
    to_left2 = hop(kvb.at[E], F, left, 7)

    lane = lax.broadcasted_iota(jnp.int32, (PAGE, n_seq * PAGE), 1)
    sub = lax.broadcasted_iota(jnp.int32, (PAGE, n_seq * PAGE), 0)
    same_token = (lane % PAGE) == sub
    lane_owner = lane // PAGE
    narrow = lax.broadcasted_iota(jnp.int32, (1, 128), 1)
    slots = jnp.full((1, 128), -1, jnp.int32)
    for j in range(PAGES):
        slot = slot_ref[j]
        pick[j * PAGE : (j + 1) * PAGE, :] = jnp.where(
            jnp.logical_and(same_token, lane_owner == slot // PAGES), 1.0, 0.0
        ).astype(BF16)
        slots = jnp.where(narrow == j, slot, slots)
    row[...] = slots
    own_copy.wait()
    pl.semaphore_wait(barrier, NZ - 1 + NP - 1 + 1)
    for k in range(4):
        rows_up[k].start()
        pl.when(last)(step1_last[k].start)
        pl.when(jnp.logical_not(last))(step1[k].start)
        pl.when(first)(extra[k].start)

    for c, outgoing in ((0, send_k), (1, send_v)):
        outgoing[...] = lax.dot_general(
            pick[...], own[c], (((0,), (0,)), ((), ())), preferred_element_type=F32
        ).astype(BF16).reshape(NZ, NP, PAGE, -1)

    stage2 = []

    def start_values():
        for copy in stage1_v:
            copy.start()

    def pass_values():
        for k, peer in enumerate(p_peers):
            remote(send_v.at[:, peer], mid_v.at[:, peer], v1_send.at[k], v1_recv.at[peer], right).wait_recv()
        local1[2].wait()
        local2[0].start()
        for k, peer in enumerate(z_peers):
            stage2.append(remote(mid_v.at[peer], got_v.at[:, z], v2_send.at[k], v2_recv.at[z], peer * NP + p))
            stage2[-1].start()

    def pass_keys():
        for k, peer in enumerate(z_peers):
            remote(send_k.at[peer], mid_k.at[:, peer], k1_send.at[k], k1_recv.at[peer], right).wait_recv()
            remote(row, tab1.at[peer], t1_send.at[k], t1_recv.at[peer], right).wait_recv()
        local1[0].wait()
        local1[1].wait()
        local2[1].start()
        local2[2].start()
        for k, peer in enumerate(p_peers):
            stage2.append(remote(mid_k.at[peer], got_k.at[p], k2_send.at[k], k2_recv.at[p], z * NP + peer))
            stage2[-1].start()
            stage2.append(remote(tab1, tab2.at[p], t2_send.at[k], t2_recv.at[p], z * NP + peer))
            stage2[-1].start()

    local2 = [
        pltpu.make_async_copy(mid_v.at[z], got_v.at[:, z], loc_sem.at[3]),
        pltpu.make_async_copy(mid_k.at[p], got_k.at[p], loc_sem.at[4]),
        pltpu.make_async_copy(tab1, tab2.at[p], loc_sem.at[5]),
    ]
    stage1 = []
    for k, peer in enumerate(z_peers):
        stage1.append(remote(send_k.at[peer], mid_k.at[:, z], k1_send.at[k], k1_recv.at[z], peer * NP + p))
        stage1.append(remote(row, tab1.at[z], t1_send.at[k], t1_recv.at[z], peer * NP + p))
    stage1_v = [
        remote(send_v.at[:, peer], mid_v.at[:, p], v1_send.at[k], v1_recv.at[p], z * NP + peer)
        for k, peer in enumerate(p_peers)
    ]
    local1 = [
        pltpu.make_async_copy(send_k.at[z], mid_k.at[:, z], loc_sem.at[0]),
        pltpu.make_async_copy(row, tab1.at[z], loc_sem.at[1]),
        pltpu.make_async_copy(send_v.at[:, p], mid_v.at[:, p], loc_sem.at[2]),
    ]
    for copy in stage1 + local1:
        copy.start()
    start_values()

    to_exp2 = math.log2(math.e) / math.sqrt(HEAD)
    tokens = own.shape[1]
    heads_kv = heads // GROUP

    def absorb(block, initial):
        for g in range(heads_kv):
            mix[g, :, :HEAD] = block[1, :, g * HEAD : (g + 1) * HEAD]

            def one(i, _):
                head = g * GROUP + i
                score = lax.dot_general(
                    q_buf[head], block[0, :, g * HEAD : (g + 1) * HEAD],
                    (((1,), (1,)), ((), ())), preferred_element_type=F32,
                ) * to_exp2
                if initial:
                    causal = lax.broadcasted_iota(jnp.int32, (tokens, tokens), 1) <= lax.broadcasted_iota(
                        jnp.int32, (tokens, tokens), 0)
                    score = jnp.where(causal, score, LOW)
                    new_top = jnp.broadcast_to(jnp.max(score, axis=1, keepdims=True), (tokens, HEAD))
                else:
                    old_top = top[head]
                    new_top = jnp.maximum(old_top, jnp.max(score, axis=1, keepdims=True))
                weight = jnp.exp2(score - jnp.concatenate([new_top, new_top], axis=1)).astype(BF16)
                mixed = jnp.dot(weight, mix[g], preferred_element_type=F32)
                top[head] = new_top
                if initial:
                    acc[head] = mixed
                else:
                    fade = jnp.exp2(old_top - new_top)
                    acc[head] = acc[head] * jnp.concatenate([fade, fade], axis=1) + mixed
                return 0

            lax.fori_loop(0, GROUP, one, 0, unroll=True)

    def absorb_slot(slot, distance):
        pl.when(s >= distance)(lambda: absorb(kvb.at[slot], False))


    def from_row(k):
        arrived(C, k)
        to_left[k].start()
        to_right[k].start()

    for k in range(4):
        @pl.when(first)
        def _():
            arrived(O, k)
            to_z[k].start()

        @pl.when(jnp.logical_not(first))
        def _():
            arrived(A, k)
            pl.when(last)(to_z2[k].start)
            pl.when(jnp.logical_not(last))(step2[k].start)

        if k >= 1:
            from_row(k - 1)
    from_row(3)

    for copy in q_copies:
        copy.wait()
    mix[:, :, HEAD:] = jnp.ones((heads_kv, tokens, HEAD), BF16)
    absorb(own, True)
    for k in range(4):
        @pl.when(first)
        def _():
            arrived(A, k)
            step2[k].start()

        @pl.when(last)
        def _():
            arrived(O2, k)
            step2_old[k].start()

    pass_values()
    absorb_slot(C, 4)
    pass_keys()

    for k in range(4):
        arrived(E, k)
        to_left2[k].start()

    absorb_slot(A, jnp.where(first, 5, 1))

    @pl.when(last)
    def _():
        for k in range(4):
            arrived(G, k)

    absorb_slot(jnp.where(last, G, E), 3)
    for slot, distance in (
        (B, jnp.where(upper, 2, 6)),
        (D, jnp.where(first, 1, 5)),
        (F, jnp.where(upper, 6, 2)),
    ):
        for k in range(4):
            arrived(slot, k)
        absorb_slot(slot, distance)

    for i in range(heads):
        o_ref[:, i * HEAD : (i + 1) * HEAD] = (acc[i, :, :HEAD] / acc[i, :, HEAD:]).astype(BF16)

    for k, peer in enumerate(z_peers):
        remote(mid_v.at[peer], got_v.at[:, peer], v2_send.at[k], v2_recv.at[peer], right).wait_recv()
    for k, peer in enumerate(p_peers):
        remote(mid_k.at[peer], got_k.at[peer], k2_send.at[k], k2_recv.at[peer], right).wait_recv()
        remote(tab1, tab2.at[peer], t2_send.at[k], t2_recv.at[peer], right).wait_recv()
    for copy in local2:
        copy.wait()
    wide = lax.broadcasted_iota(jnp.int32, (PAGE, PAGES * PAGE), 1)
    wide_token = (wide % PAGE) == lax.broadcasted_iota(jnp.int32, (PAGE, PAGES * PAGE), 0)
    wide_slot = wide // PAGE
    for source in range(n_seq):
        named = jnp.broadcast_to(tab2[source // NZ, source % NZ], (PAGE, 128))
        mine = jnp.where(named // PAGES == s, named % PAGES + 1, 0)
        within = jnp.sum(mine, axis=1, keepdims=True) - 1
        place[source * PAGE : (source + 1) * PAGE, :] = jnp.where(
            jnp.logical_and(wide_token, wide_slot == within), 1.0, 0.0
        ).astype(BF16)
    for c, pages in ((0, got_k), (1, got_v)):
        pool_ref[c] = lax.dot_general(
            place[...], pages[...].reshape(n_seq * PAGE, -1), (((0,), (0,)), ((), ())), preferred_element_type=F32
        ).astype(BF16)

    for k in range(4):
        rows_up[k].wait_send()
        pl.when(first)(to_z[k].wait_send)
        pl.when(last)(to_z2[k].wait_send)
        step1[k].wait_send()
        pl.when(first)(extra[k].wait_send)
        step2[k].wait_send()
        to_right[k].wait_send()
        to_left[k].wait_send()
        to_left2[k].wait_send()
    for copy in stage1 + stage1_v + stage2:
        copy.wait_send()


def body(queries, new_key_value, page_slot):
    tokens, features = queries.shape
    width = new_key_value.shape[2]
    heads = features // HEAD
    n_seq = NP * NZ
    kv_block = (2, tokens, width)
    dma = pltpu.SemaphoreType.DMA
    attended, pool = pl.pallas_call(
        kernel,
        name="layer",
        out_shape=(
            jax.ShapeDtypeStruct((tokens, features), BF16),
            jax.ShapeDtypeStruct(kv_block, BF16),
        ),
        in_specs=[
            pl.BlockSpec(memory_space=pltpu.SMEM),
            pl.BlockSpec(memory_space=pl.ANY),
            pl.BlockSpec(memory_space=pl.ANY),
        ],
        out_specs=(
            pl.BlockSpec(memory_space=pltpu.VMEM),
            pl.BlockSpec(memory_space=pltpu.VMEM),
        ),
        scratch_shapes=[
            pltpu.VMEM((heads, tokens, HEAD), BF16),
            pltpu.VMEM(kv_block, BF16),
            pltpu.VMEM((9,) + kv_block, BF16),
            pltpu.VMEM((heads, tokens, 2 * HEAD), F32),
            pltpu.VMEM((heads, tokens, HEAD), F32),
            pltpu.VMEM((width // HEAD, tokens, 2 * HEAD), BF16),
            pltpu.VMEM((PAGES * PAGE, n_seq * PAGE), BF16),
            *[pltpu.VMEM((NP, NP, PAGE, width), BF16)] * 6,
            pltpu.VMEM((1, 128), jnp.int32),
            pltpu.VMEM((NZ, 1, 128), jnp.int32),
            pltpu.VMEM((NP, NZ, 1, 128), jnp.int32),
            pltpu.VMEM((n_seq * PAGE, PAGES * PAGE), BF16),
            dma((heads,)), dma, dma((6,)), dma((9, 4)), dma((9, 4)),
            *[dma((NP,))] * 12,
        ],
        compiler_params=pltpu.CompilerParams(
            collective_id=0, has_side_effects=True, vmem_limit_bytes=60 * 1024 * 1024
        ),
    )(page_slot, queries, new_key_value)
    return attended, pool.reshape(2, PAGES, PAGE, width)


def solution(mesh):
    return jax.shard_map(
        body,
        mesh=mesh,
        in_specs=(P("seq", "tp"), P(None, "seq", "tp"), P("seq")),
        out_specs=(P("seq", "tp"), P(None, "seq", None, "tp")),
        check_vma=False,
    )
```
